256 devices in a mesh: dp: 4 (over x), row: 8 (over z_lo, core), col: 8 (over z_hi, y).
Axes of the slice: x: 4, y: 4, z: 8 (z_hi: 2, z_lo: 4; z = z_hi * 4 + z_lo), core: 2. Of those that a mesh axis runs over, the one named last changes fastest.
Arguments:
- tokens: bfloat16 [4096, 8192], P(('dp', 'col'), 'row'), may hold values from -6 to 6
- gate_weight: bfloat16 [8192, 14336], P('row', ('dp', 'col')), may hold values from -0.0625 to 0.0625
- up_weight: bfloat16 [8192, 14336], P('row', ('dp', 'col')), may hold values from -0.0625 to 0.0625
- down_weight: bfloat16 [14336, 8192], P(('dp', 'col'), 'row'), may hold values from -0.046875 to 0.046875
Outputs:
- mixed: bfloat16 [4096, 8192], P(('dp', 'col'), 'row')
The draws below stay inside these ranges and needn't reach their ends.
All inputs are finite; a program needn't handle non-finite values.
Results may differ from the reference program's by a relative error of at most 0.03.
Values may be sent and summed in bfloat16 or wider, within the bound.
A program may use at most 64 MiB of HBM per device.

```python
import jax
import jax.numpy as jnp
from jax import lax

D = 8192
FF = 14336
TOKENS = 4096
N_ROW = 8


def steps_of(stream_key, dims, split, least, high):
    level = 1.0
    for dim, blocks in split:
        heights = jax.random.uniform(jax.random.fold_in(jax.random.fold_in(stream_key, 6), dim), (blocks,), jnp.float32, least / len(split), high / len(split))
        level = level * jnp.repeat(jnp.exp(heights), dims[dim] // blocks).reshape((-1,) + (1,) * (len(dims) - 1 - dim))
    return level


def gaussian(rng, dims, deviation, bound, cuts=(), dtype=jnp.bfloat16):
    values = jax.random.normal(rng, dims, jnp.float32) * deviation
    if len(cuts) > 0:
        values = steps_of(rng, dims, cuts, -0.22, 0.18) * values
    return jnp.clip(values, min=-bound, max=bound).astype(dtype)


def setup_inputs(seed: int = 0) -> dict:
    seeds = jax.random.split(jax.random.key(seed), 5)
    return {
        "tokens": gaussian(seeds[0], (TOKENS, D), 1.0, 6.0, ((0, 32), (1, 8))),
        "gate_weight": gaussian(seeds[1], (D, FF), D ** -0.5, 0.0625, ((0, 8), (1, 32))),
        "up_weight": gaussian(seeds[2], (D, FF), D ** -0.5, 0.0625, ((0, 8), (1, 32))),
        "down_weight": gaussian(seeds[3], (FF, D), FF ** -0.5, 0.046875, ((0, 32), (1, 8))),
    }


def reference(tokens, gate_weight, up_weight, down_weight):
    block_width = D // N_ROW
    gate_sum = jnp.zeros((TOKENS, FF), jnp.float32)
    up_sum = jnp.zeros((TOKENS, FF), jnp.float32)
    for position in range(N_ROW):
        lower = position * block_width
        row_block = tokens[:, lower:lower + block_width]
        gate_part = jnp.dot(row_block, gate_weight[lower:lower + block_width], preferred_element_type=jnp.float32).astype(jnp.bfloat16)
        up_part = jnp.dot(row_block, up_weight[lower:lower + block_width], preferred_element_type=jnp.float32).astype(jnp.bfloat16)
        gate_part, up_part = lax.optimization_barrier((gate_part, up_part))
        gate_sum = gate_sum + gate_part.astype(jnp.float32)
        up_sum = up_sum + up_part.astype(jnp.float32)
    hidden = (jax.nn.silu(gate_sum) * up_sum).astype(jnp.bfloat16)
    return jnp.dot(hidden, down_weight, preferred_element_type=jnp.float32).astype(jnp.bfloat16)
```

```python
import functools

import jax
import jax.numpy as jnp
from jax import lax
from jax.experimental import pallas as pl
from jax.experimental.pallas import tpu as pltpu
from jax.sharding import PartitionSpec as P

MESH = pl.DeviceIdType.MESH
F32 = jnp.float32
BF16 = jnp.bfloat16

CHUNKS = 2
BLOCK = 128
HALF = BLOCK // CHUNKS // 2
UNITS = 448
MAIN = 384
PACKED = 896
PADDED = 512
WIDTH = 1024
MESSAGES = 36


def kernel(tokens_ref, gate_ref, up_ref, down_ref, out_ref,
           tok, w, d, part, pair, chain_in, chain_out, hid, term,
           in_far, in_near, in_far2, in_near2, z_send, z_in,
           send_sem, recv_sem, local_sem):
    x = lax.axis_index("dp")
    row = lax.axis_index("row")
    col = lax.axis_index("col")
    z, core = row // 2, row % 2
    zh, y = col // 4, col % 4

    def shift(value, by):
        return lax.rem(value + (by + 4), 4)

    core_peer = {"row": row + 1 - 2 * core}
    zh_peer = {"col": (1 - zh) * 4 + y}
    x_peer = {1: {"dp": shift(x, 1)}, -1: {"dp": shift(x, -1)}}
    y_peer = {1: {"col": zh * 4 + shift(y, 1)}, -1: {"col": zh * 4 + shift(y, -1)}}

    barrier = pltpu.get_barrier_semaphore()
    for peer in (core_peer, zh_peer, x_peer[1], x_peer[-1], y_peer[1], y_peer[-1]):
        pl.semaphore_signal(barrier, inc=1, device_id=peer, device_id_type=MESH)

    @pl.when(z > 0)
    def _():
        pl.semaphore_signal(barrier, inc=1, device_id={"row": row - 2}, device_id_type=MESH)

    @pl.when(z < 3)
    def _():
        pl.semaphore_signal(barrier, inc=1, device_id={"row": row + 2}, device_id_type=MESH)

    at_end = jnp.logical_or(z == 0, z == 3)

    @pl.when(at_end)
    def _():
        pl.semaphore_wait(barrier, 7)

    @pl.when(jnp.logical_not(at_end))
    def _():
        pl.semaphore_wait(barrier, 8)

    sent = []

    def copy(src, dst, index, peer):
        return pltpu.make_async_remote_copy(
            src_ref=src, dst_ref=dst, send_sem=send_sem.at[index], recv_sem=recv_sem.at[index],
            device_id=peer, device_id_type=MESH)

    def send(src, dst, index, peer, guard=None):
        copy(src, dst, index, peer).start()
        sent.append((src, dst, index, peer, guard))

    def arrived(dst, index, peer):
        copy(dst, dst, index, peer).wait_recv()

    tasks = []

    def add(time, run, guard=None):
        tasks.append((time, len(tasks), run, guard))

    def one(c, o):
        base = (c * 2 + o) * MESSAGES
        first, second = (x, y) if o == 0 else (y, x)
        first_peer, second_peer = (x_peer, y_peer) if o == 0 else (y_peer, x_peer)
        lo = (c * 2 + o) * HALF
        mine = tokens_ref.at[pl.ds(lo, HALF)]
        here = tok.at[c, o]
        f = {k: shift(first, k) for k in (-1, 0, 1, 2)}
        s = {k: shift(second, k) for k in (-1, 0, 1, 2)}
        local = pltpu.make_async_copy(mine, here.at[s[0], f[0], zh], local_sem.at[c * 2 + o])
        t = lambda stage: TIMES[stage][c]

        def begin():
            send(mine, here.at[s[0], f[0], zh], base + 0, zh_peer)
            for i, way in enumerate((1, -1)):
                send(mine, here.at[s[0], f[0], zh], base + 1 + i, first_peer[way])
            local.start()

        def other_half():
            block = here.at[s[0], f[0], 1 - zh]
            arrived(block, base + 0, zh_peer)
            for i, way in enumerate((1, -1)):
                send(block, block, base + 3 + i, first_peer[way])

        def forward_own():
            block = here.at[s[0], f[-1], zh]
            arrived(block, base + 1, first_peer[-1])
            send(block, block, base + 5, first_peer[1])

        def forward_other():
            block = here.at[s[0], f[1], 1 - zh]
            arrived(block, base + 4, first_peer[1])
            send(block, block, base + 6, first_peer[-1])

        def second_axis():
            arrived(here.at[s[0], f[1], zh], base + 2, first_peer[1])
            arrived(here.at[s[0], f[-1], 1 - zh], base + 3, first_peer[-1])
            arrived(here.at[s[0], f[2], zh], base + 5, first_peer[-1])
            arrived(here.at[s[0], f[2], 1 - zh], base + 6, first_peer[1])
            local.wait()
            for i, way in enumerate((1, -1)):
                send(here.at[s[0]], here.at[s[0]], base + 7 + i, second_peer[way])

        def forward_second():
            arrived(here.at[s[-1]], base + 7, second_peer[-1])
            block = here.at[s[-1], 0:2]
            send(block, block, base + 9, second_peer[1])
            arrived(here.at[s[1]], base + 8, second_peer[1])
            block = here.at[s[1], 2:4]
            send(block, block, base + 10, second_peer[-1])

        add(t("begin"), begin)
        add(t("other_half"), other_half)
        add(t("forward_own"), forward_own)
        add(t("forward_other"), forward_other)
        add(t("second_axis"), second_axis)
        add(t("forward_second"), forward_second)

        p = z if o == 0 else 3 - z
        on = [p == position for position in range(4)]
        onward = {"row": row + 2} if o == 0 else {"row": row - 2}
        backward = {"row": row - 2} if o == 0 else {"row": row + 2}

        def tile(k):
            order = ORDER[c].index(k)
            key = k if k < 3 else -1
            rows = 4 * HALF
            own = part.at[c, o, k, :, core]
            away = part.at[c, o, k, :, 1 - core]
            pair_in = pair.at[c, o, k]
            incoming = chain_in.at[c, o, k]
            outgoing = chain_out.at[c, o, k]
            hidden = hid.at[c, o, k, core]
            hidden_away = hid.at[c, o, k, 1 - core]

            def gate_up():
                if k == 2:
                    arrived(here.at[s[2], 0:2], base + 9, second_peer[-1])
                    arrived(here.at[s[2], 2:4], base + 10, second_peer[1])
                a = here[s[key]].reshape(2 * rows, WIDTH)
                both = jnp.dot(a, w[...], preferred_element_type=F32).astype(BF16)
                part[c, o, k] = both.reshape(4, 2, HALF, PACKED)
                send(away, pair_in, base + 11 + k, core_peer)

            def total(with_chain):
                value = own[...].astype(F32).reshape(rows, PACKED) + pair_in[...].astype(F32).reshape(rows, PACKED)
                if with_chain:
                    value = value + incoming[...].astype(F32)
                return value

            def link(position):
                def run():
                    arrived(pair_in, base + 11 + k, core_peer)
                    if position:
                        arrived(incoming, base + 15 + k, backward)
                    value = total(position > 0)
                    if position < 3:
                        outgoing[...] = value.astype(BF16)
                        send(outgoing, incoming, base + 15 + k, onward, on[position])
                    else:
                        g, u = value[:, :MAIN], value[:, MAIN:2 * MAIN]
                        last = value[:, 2 * MAIN:]
                        turned = pltpu.roll(last, 64, 1)
                        lane = lax.broadcasted_iota(jnp.int32, last.shape, 1)
                        hidden[:, :MAIN] = (jax.nn.silu(g) * u).astype(BF16)
                        hidden[:, MAIN:] = jnp.where(lane < 64, jax.nn.silu(last) * turned, 0.0).astype(BF16)
                        send(hidden, hidden, base + 19 + k, backward, on[position])
                        send(hidden, hidden, base + 23 + k, core_peer, on[position])
                return run

            def spread(position):
                def run():
                    arrived(hidden, base + 19 + k, onward)
                    if position:
                        send(hidden, hidden, base + 19 + k, backward, on[position])
                    send(hidden, hidden, base + 23 + k, core_peer, on[position])
                return run

            def down():
                arrived(hidden_away, base + 23 + k, core_peer)
                a = hid[c, o, k].reshape(2 * rows, PADDED)
                term[c, o, k] = jnp.dot(a, d[...], preferred_element_type=F32).astype(BF16).reshape(2, 4, HALF, WIDTH)

            def out_far():
                for i, way in enumerate((1, -1)):
                    send(term.at[c, o, 2, i], in_far.at[c, o, i], base + 27 + i, second_peer[way])

            def out_near():
                i, way = (0, 1) if k == 1 else (1, -1)
                arrived(in_far.at[c, o, i], base + 27 + i, second_peer[-way])
                term[c, o, k, i] = (term[c, o, k, i].astype(F32) + in_far[c, o, i].astype(F32)).astype(BF16)
                send(term.at[c, o, k], in_near.at[c, o, i], base + 29 + i, second_peer[way])

            add(TIMES["gate_up"][c][order], gate_up)
            for position in range(4):
                add(TIMES["link"][c][order] + HOP * position, link(position), on[position])
            for position in (2, 1, 0):
                add(TIMES["link"][c][order] + HOP * 3 + SPREAD * (3 - position), spread(position), on[position])
            at = TIMES["down"][c][order]
            add(at, down)
            if k == 2:
                add(at + 0.1, out_far)
            elif k:
                add(max(at, TIMES["down"][c][ORDER[c].index(2)] + FAR) + 0.2, out_near)

        for k in ORDER[c]:
            tile(k)

        def out_second():
            for i, way in enumerate((1, -1)):
                arrived(in_near.at[c, o, i], base + 29 + i, second_peer[-way])
            value = term[c, o, 0].astype(F32) + in_near[c, o, 0].astype(F32) + in_near[c, o, 1].astype(F32)
            term[c, o, 0] = value.astype(BF16)
            for i, way in enumerate((1, -1)):
                send(term.at[c, o, 0, i, f[2]], in_far2.at[c, o, i], base + 31 + i, first_peer[way])

        def out_first():
            for i, way in enumerate((1, -1)):
                arrived(in_far2.at[c, o, i], base + 31 + i, first_peer[-way])
                block = term.at[c, o, 0, i, f[way]]
                block[...] = (block[...].astype(F32) + in_far2[c, o, i].astype(F32)).astype(BF16)
                send(term.at[c, o, 0, :, f[way]], in_near2.at[c, o, i], base + 33 + i, first_peer[way])

        def out_zh():
            for i, way in enumerate((1, -1)):
                arrived(in_near2.at[c, o, i], base + 33 + i, first_peer[-way])
            z_send[c, o] = (term[c, o, 0, :, f[0]].astype(F32) + in_near2[c, o, 0].astype(F32)
                            + in_near2[c, o, 1].astype(F32)).astype(BF16)
            send(z_send.at[c, o, 1 - zh], z_in.at[c, o], base + 35, zh_peer)

        def out_end():
            arrived(z_in.at[c, o], base + 35, zh_peer)
            out_ref[pl.ds(lo, HALF)] = (z_send[c, o, zh].astype(F32) + z_in[c, o].astype(F32)).astype(BF16)

        add(t("out_second"), out_second)
        add(t("out_first"), out_first)
        add(t("out_zh"), out_zh)
        add(t("out_end"), out_end)

    def pack():
        w[:, :MAIN] = gate_ref[:, :MAIN]
        w[:, MAIN:2 * MAIN] = up_ref[:, :MAIN]
        w[:, 2 * MAIN:] = jnp.concatenate((gate_ref[:, MAIN:], up_ref[:, MAIN:]), axis=1)
        d[:UNITS] = down_ref[...]
        d[UNITS:] = jnp.zeros((PADDED - UNITS, WIDTH), BF16)

    add(1.0, pack)
    for c in range(CHUNKS):
        for o in range(2):
            one(c, o)

    for _, _, run, guard in sorted(tasks, key=lambda task: task[:2]):
        if guard is None:
            run()
        else:
            pl.when(guard)(run)

    for src, dst, index, peer, guard in sent:
        def finish(item=(src, dst, index, peer)):
            copy(*item).wait_send()

        if guard is None:
            finish()
        else:
            pl.when(guard)(finish)


HOP = 7.0
SPREAD = 3.5
FAR = 8.0
ORDER = ((0, 1, 3, 2), (2, 1, 3, 0))
TIMES = {
    "begin": (0, 14),
    "other_half": (6, 20),
    "forward_own": (4, 18.5),
    "forward_other": (9, 22),
    "second_axis": (13, 27.5),
    "forward_second": (26, 46),
    "gate_up": ((14, 27, 28, 34), (53, 54, 55, 56)),
    "link": ((16, 28.5, 33, 38), (55, 58, 63, 68)),
    "down": ((49, 61, 66, 71), (89, 92, 97, 102)),
    "out_second": (92.5, 116),
    "out_first": (96, 120),
    "out_zh": (99, 124),
    "out_end": (105, 130),
}


def on_device(tokens, gate_weight, up_weight, down_weight):
    vmem = pl.BlockSpec(memory_space=pltpu.VMEM)
    c2 = (CHUNKS, 2)
    messages = CHUNKS * 2 * MESSAGES
    return pl.pallas_call(
        kernel,
        out_shape=jax.ShapeDtypeStruct(tokens.shape, BF16),
        in_specs=[vmem] * 4,
        out_specs=vmem,
        scratch_shapes=[
            pltpu.VMEM(c2 + (4, 4, 2, HALF, WIDTH), BF16),
            pltpu.VMEM((WIDTH, PACKED), BF16),
            pltpu.VMEM((PADDED, WIDTH), BF16),
            pltpu.VMEM(c2 + (4, 4, 2, HALF, PACKED), BF16),
            pltpu.VMEM(c2 + (4, 4, HALF, PACKED), BF16),
            pltpu.VMEM(c2 + (4, 4 * HALF, PACKED), BF16),
            pltpu.VMEM(c2 + (4, 4 * HALF, PACKED), BF16),
            pltpu.VMEM(c2 + (4, 2, 4 * HALF, PADDED), BF16),
            pltpu.VMEM(c2 + (4, 2, 4, HALF, WIDTH), BF16),
            pltpu.VMEM(c2 + (2, 4, HALF, WIDTH), BF16),
            pltpu.VMEM(c2 + (2, 2, 4, HALF, WIDTH), BF16),
            pltpu.VMEM(c2 + (2, HALF, WIDTH), BF16),
            pltpu.VMEM(c2 + (2, 2, HALF, WIDTH), BF16),
            pltpu.VMEM(c2 + (2, HALF, WIDTH), BF16),
            pltpu.VMEM(c2 + (HALF, WIDTH), BF16),
            pltpu.SemaphoreType.DMA((messages,)),
            pltpu.SemaphoreType.DMA((messages,)),
            pltpu.SemaphoreType.DMA((CHUNKS * 2,)),
        ],
        compiler_params=pltpu.CompilerParams(
            collective_id=0, has_side_effects=True, vmem_limit_bytes=63 * 1024 * 1024),
    )(tokens, gate_weight, up_weight, down_weight)


def solution(mesh):
    return jax.shard_map(
        on_device,
        mesh=mesh,
        in_specs=(
            P(("dp", "col"), "row"),
            P("row", ("dp", "col")),
            P("row", ("dp", "col")),
            P(("dp", "col"), "row"),
        ),
        out_specs=P(("dp", "col"), "row"),
        check_vma=False,
    )
```

```python
import functools

import jax
import jax.numpy as jnp
from jax import lax
from jax.experimental import pallas as pl
from jax.experimental.pallas import tpu as pltpu
from jax.sharding import PartitionSpec as P

MESH = pl.DeviceIdType.MESH
F32 = jnp.float32
BF16 = jnp.bfloat16

CHUNKS = 4
BLOCK = 128
HALF = BLOCK // CHUNKS // 2
UNITS = 448
MAIN = 384
PACKED = 896
PADDED = 512
WIDTH = 1024
MESSAGES = 36


def kernel(tokens_ref, gate_ref, up_ref, down_ref, out_ref,
           tok, w, d, part, pair, chain_in, chain_out, hid, term,
           in_far, in_near, in_far2, in_near2, z_send, z_in,
           send_sem, recv_sem, local_sem):
    x = lax.axis_index("dp")
    row = lax.axis_index("row")
    col = lax.axis_index("col")
    z, core = row // 2, row % 2
    zh, y = col // 4, col % 4

    def shift(value, by):
        return lax.rem(value + (by + 4), 4)

    core_peer = {"row": row + 1 - 2 * core}
    zh_peer = {"col": (1 - zh) * 4 + y}
    def ring(by_x, by_y):
        return {"dp": lax.rem(x + (by_x + 4), 4), "col": zh * 4 + lax.rem(y + (by_y + 4), 4)}

    near = z // 2

    barrier = pltpu.get_barrier_semaphore()
    for peer in (core_peer, zh_peer, ring(1, 0), ring(-1, 0), ring(0, 1), ring(0, -1)):
        pl.semaphore_signal(barrier, inc=1, device_id=peer, device_id_type=MESH)

    @pl.when(z > 0)
    def _():
        pl.semaphore_signal(barrier, inc=1, device_id={"row": row - 2}, device_id_type=MESH)

    @pl.when(z < 3)
    def _():
        pl.semaphore_signal(barrier, inc=1, device_id={"row": row + 2}, device_id_type=MESH)

    at_end = jnp.logical_or(z == 0, z == 3)

    @pl.when(at_end)
    def _():
        pl.semaphore_wait(barrier, 7)

    @pl.when(jnp.logical_not(at_end))
    def _():
        pl.semaphore_wait(barrier, 8)

    sent = []

    def copy(src, dst, index, peer):
        place = index[0] + index[1]
        return pltpu.make_async_remote_copy(
            src_ref=src, dst_ref=dst, send_sem=send_sem.at[place], recv_sem=recv_sem.at[place],
            device_id=peer, device_id_type=MESH)

    def send(src, dst, index, peer, guard=None):
        copy(src, dst, index, peer).start()
        sent.append((src, dst, index, peer, guard))

    def arrived(dst, index, peer):
        copy(dst, dst, index, peer).wait_recv()

    tasks = []

    def add(run, guard=None):
        tasks.append((run, guard))

    def one(c, n):
        o = n + near - 2 * n * near
        swap = o
        base = (c * 2 + o) * MESSAGES
        first, second = x + swap * (y - x), y + swap * (x - y)
        first_peer = {way: ring((1 - swap) * way, swap * way) for way in (1, -1)}
        second_peer = {way: ring(swap * way, (1 - swap) * way) for way in (1, -1)}
        lo = pl.multiple_of((c * 2 + o) * HALF, HALF)
        mine = tokens_ref.at[pl.ds(lo, HALF)]
        here = tok.at[c, o]
        f = {k: shift(first, k) for k in (-1, 0, 1, 2)}
        s = {k: shift(second, k) for k in (-1, 0, 1, 2)}
        local = pltpu.make_async_copy(mine, here.at[s[0], f[0], zh], local_sem.at[c * 2 + o])

        def begin():
            send(mine, here.at[s[0], f[0], zh], (base, 0), zh_peer)
            for i, way in enumerate((1, -1)):
                send(mine, here.at[s[0], f[0], zh], (base, 1 + i), first_peer[way])
            local.start()

        def other_half():
            block = here.at[s[0], f[0], 1 - zh]
            arrived(block, (base, 0), zh_peer)
            for i, way in enumerate((1, -1)):
                send(block, block, (base, 3 + i), first_peer[way])

        def forward_own():
            block = here.at[s[0], f[-1], zh]
            arrived(block, (base, 1), first_peer[-1])
            send(block, block, (base, 5), first_peer[1])

        def forward_other():
            block = here.at[s[0], f[1], 1 - zh]
            arrived(block, (base, 4), first_peer[1])
            send(block, block, (base, 6), first_peer[-1])

        def second_axis():
            arrived(here.at[s[0], f[1], zh], (base, 2), first_peer[1])
            arrived(here.at[s[0], f[-1], 1 - zh], (base, 3), first_peer[-1])
            arrived(here.at[s[0], f[2], zh], (base, 5), first_peer[-1])
            arrived(here.at[s[0], f[2], 1 - zh], (base, 6), first_peer[1])
            local.wait()
            for i, way in enumerate((1, -1)):
                send(here.at[s[0]], here.at[s[0]], (base, 7 + i), second_peer[way])

        def forward_second(way):
            lower = 0 if way == 1 else 2

            def run():
                arrived(here.at[s[-way]], (base, (7 if way == 1 else 8)), second_peer[-way])
                block = here.at[s[-way], lower:lower + 2]
                send(block, block, (base, (9 if way == 1 else 10)), second_peer[way])

            return run

        add(begin)
        add(other_half)
        add(forward_own)
        add(forward_other)
        add(second_axis)
        add(forward_second(1))
        add(forward_second(-1))

        p = z + o * (3 - 2 * z)
        on = [p == position for position in range(4)]
        onward, backward = {"row": row + 2 - 4 * o}, {"row": row - 2 + 4 * o}

        def tile(k):
            key = k if k < 3 else -1
            rows = 4 * HALF
            own = part.at[c, o, k, :, core]
            away = part.at[c, o, k, :, 1 - core]
            pair_in = pair.at[c, o, k]
            incoming = chain_in.at[c, o, k]
            outgoing = chain_out.at[c, o, k]
            hidden = hid.at[c, o, k, core]
            hidden_away = hid.at[c, o, k, 1 - core]

            def gate_up():
                if k == 2:
                    arrived(here.at[s[2], 0:2], (base, 9), second_peer[-1])
                    arrived(here.at[s[2], 2:4], (base, 10), second_peer[1])
                a = here[s[key]].reshape(2 * rows, WIDTH)
                both = jnp.dot(a, w[...], preferred_element_type=F32).astype(BF16)
                part[c, o, k] = both.reshape(4, 2, HALF, PACKED)
                send(away, pair_in, (base, 11 + k), core_peer)

            def total(with_chain):
                value = own[...].astype(F32).reshape(rows, PACKED) + pair_in[...].astype(F32).reshape(rows, PACKED)
                if with_chain:
                    value = value + incoming[...].astype(F32)
                return value

            def link(position):
                def run():
                    arrived(pair_in, (base, 11 + k), core_peer)
                    if position:
                        arrived(incoming, (base, 15 + k), backward)
                    value = total(position > 0)
                    if position < 3:
                        outgoing[...] = value.astype(BF16)
                        send(outgoing, incoming, (base, 15 + k), onward, on[position])
                    else:
                        g, u = value[:, :MAIN], value[:, MAIN:2 * MAIN]
                        last = value[:, 2 * MAIN:]
                        turned = pltpu.roll(last, 64, 1)
                        lane = lax.broadcasted_iota(jnp.int32, last.shape, 1)
                        hidden[:, :MAIN] = (jax.nn.silu(g) * u).astype(BF16)
                        hidden[:, MAIN:] = jnp.where(lane < 64, jax.nn.silu(last) * turned, 0.0).astype(BF16)
                        send(hidden, hidden, (base, 19 + k), backward, on[position])
                        send(hidden, hidden, (base, 23 + k), core_peer, on[position])
                return run

            def spread(position):
                def run():
                    arrived(hidden, (base, 19 + k), onward)
                    if position:
                        send(hidden, hidden, (base, 19 + k), backward, on[position])
                    send(hidden, hidden, (base, 23 + k), core_peer, on[position])
                return run

            def down():
                arrived(hidden_away, (base, 23 + k), core_peer)
                a = hid[c, o, k].reshape(2 * rows, PADDED)
                term[c, o, k] = jnp.dot(a, d[...], preferred_element_type=F32).astype(BF16).reshape(2, 4, HALF, WIDTH)

            def out_far():
                for i, way in enumerate((1, -1)):
                    send(term.at[c, o, 2, i], in_far.at[c, o, i], (base, 27 + i), second_peer[way])

            def out_near():
                i, way = (0, 1) if k == 1 else (1, -1)
                arrived(in_far.at[c, o, i], (base, 27 + i), second_peer[-way])
                term[c, o, k, i] = (term[c, o, k, i].astype(F32) + in_far[c, o, i].astype(F32)).astype(BF16)
                send(term.at[c, o, k], in_near.at[c, o, i], (base, 29 + i), second_peer[way])

            add(gate_up)
            for position in range(2 - 2 * (1 - n), 4 - 2 * (1 - n)):
                add(link(position), on[position])
            for position in (2, 1, 0):
                if position // 2 == n:
                    add(spread(position), on[position])
            add(down)
            return out_far if k == 2 else out_near

        outs = [tile(k) for k in range(4)]
        for k in (2, 1, 3):
            add(outs[k])

        def out_second():
            for i, way in enumerate((1, -1)):
                arrived(in_near.at[c, o, i], (base, 29 + i), second_peer[-way])
            value = term[c, o, 0].astype(F32) + in_near[c, o, 0].astype(F32) + in_near[c, o, 1].astype(F32)
            term[c, o, 0] = value.astype(BF16)
            for i, way in enumerate((1, -1)):
                send(term.at[c, o, 0, i, f[2]], in_far2.at[c, o, i], (base, 31 + i), first_peer[way])

        def out_first():
            for i, way in enumerate((1, -1)):
                arrived(in_far2.at[c, o, i], (base, 31 + i), first_peer[-way])
                block = term.at[c, o, 0, i, f[way]]
                block[...] = (block[...].astype(F32) + in_far2[c, o, i].astype(F32)).astype(BF16)
                send(term.at[c, o, 0, :, f[way]], in_near2.at[c, o, i], (base, 33 + i), first_peer[way])

        def out_zh():
            for i, way in enumerate((1, -1)):
                arrived(in_near2.at[c, o, i], (base, 33 + i), first_peer[-way])
            z_send[c, o] = (term[c, o, 0, :, f[0]].astype(F32) + in_near2[c, o, 0].astype(F32)
                            + in_near2[c, o, 1].astype(F32)).astype(BF16)
            send(z_send.at[c, o, 1 - zh], z_in.at[c, o], (base, 35), zh_peer)

        def out_end():
            arrived(z_in.at[c, o], (base, 35), zh_peer)
            out_ref[pl.ds(lo, HALF)] = (z_send[c, o, zh].astype(F32) + z_in[c, o].astype(F32)).astype(BF16)

        add(out_second)
        add(out_first)
        add(out_zh)
        add(out_end)

    def pack():
        w[:, :MAIN] = gate_ref[:, :MAIN]
        w[:, MAIN:2 * MAIN] = up_ref[:, :MAIN]
        w[:, 2 * MAIN:] = jnp.concatenate((gate_ref[:, MAIN:], up_ref[:, MAIN:]), axis=1)
        d[:UNITS] = down_ref[...]
        d[UNITS:] = jnp.zeros((PADDED - UNITS, WIDTH), BF16)

    for c in range(CHUNKS):
        for n in range(2):
            one(c, n)
    for place, number in enumerate(ORDER):
        if place == PACK:
            pack()
        run, guard = tasks[number]
        if guard is None:
            run()
        else:
            pl.when(guard)(run)

    for src, dst, index, peer, guard in sent:
        def finish(item=(src, dst, index, peer)):
            copy(*item).wait_send()

        if guard is None:
            finish()
        else:
            pl.when(guard)(finish)


PACK = 4
ORDER = (
    0, 38, 182, 110, 72, 216, 144, 2, 74, 112, 254, 256, 40, 1, 39, 3, 218, 146, 183, 41,
    111, 73, 4, 7, 8, 75, 184, 145, 217, 113, 255, 185, 76, 79, 80, 147, 42, 45, 9, 46,
    5, 81, 6, 13, 14, 15, 148, 151, 152, 186, 189, 219, 25, 26, 47, 114, 117, 44, 50, 51,
    118, 27, 153, 77, 97, 98, 19, 20, 257, 78, 85, 86, 99, 43, 60, 48, 49, 61, 149, 169,
    170, 52, 91, 92, 21, 150, 157, 158, 220, 223, 224, 116, 122, 115, 132, 62, 171, 55, 56, 57,
    163, 164, 258, 261, 133, 134, 93, 87, 187, 204, 205, 127, 188, 194, 119, 159, 128, 129, 206, 221,
    241, 242, 222, 229, 260, 266, 123, 124, 58, 59, 65, 63, 64, 22, 165, 199, 259, 195, 196, 135,
    235, 236, 120, 23, 24, 31, 28, 29, 53, 54, 66, 200, 201, 207, 208, 190, 191, 243, 67, 121,
    100, 130, 131, 137, 16, 17, 276, 230, 172, 125, 30, 33, 271, 18, 32, 225, 101, 102, 277, 278,
    94, 95, 96, 103, 202, 203, 209, 237, 262, 173, 174, 166, 167, 136, 139, 231, 126, 138, 88, 89,
    168, 175, 263, 105, 211, 272, 273, 90, 104, 197, 198, 210, 267, 268, 177, 68, 82, 83, 192, 193,
    160, 140, 161, 162, 176, 10, 11, 274, 275, 281, 84, 106, 12, 34, 238, 239, 240, 247, 154, 269,
    212, 279, 280, 283, 270, 282, 232, 155, 156, 178, 69, 141, 233, 234, 248, 244, 245, 246, 249, 35,
    264, 265, 284, 226, 107, 108, 213, 179, 142, 70, 227, 228, 250, 36, 214, 285, 251, 180, 286, 252,
    215, 109, 181, 143, 71, 287, 253, 37,
)


def on_device(tokens, gate_weight, up_weight, down_weight):
    vmem = pl.BlockSpec(memory_space=pltpu.VMEM)
    c2 = (CHUNKS, 2)
    messages = CHUNKS * 2 * MESSAGES
    return pl.pallas_call(
        kernel,
        out_shape=jax.ShapeDtypeStruct(tokens.shape, BF16),
        in_specs=[vmem] * 4,
        out_specs=vmem,
        scratch_shapes=[
            pltpu.VMEM(c2 + (4, 4, 2, HALF, WIDTH), BF16),
            pltpu.VMEM((WIDTH, PACKED), BF16),
            pltpu.VMEM((PADDED, WIDTH), BF16),
            pltpu.VMEM(c2 + (4, 4, 2, HALF, PACKED), BF16),
            pltpu.VMEM(c2 + (4, 4, HALF, PACKED), BF16),
            pltpu.VMEM(c2 + (4, 4 * HALF, PACKED), BF16),
            pltpu.VMEM(c2 + (4, 4 * HALF, PACKED), BF16),
            pltpu.VMEM(c2 + (4, 2, 4 * HALF, PADDED), BF16),
            pltpu.VMEM(c2 + (4, 2, 4, HALF, WIDTH), BF16),
            pltpu.VMEM(c2 + (2, 4, HALF, WIDTH), BF16),
            pltpu.VMEM(c2 + (2, 2, 4, HALF, WIDTH), BF16),
            pltpu.VMEM(c2 + (2, HALF, WIDTH), BF16),
            pltpu.VMEM(c2 + (2, 2, HALF, WIDTH), BF16),
            pltpu.VMEM(c2 + (2, HALF, WIDTH), BF16),
            pltpu.VMEM(c2 + (HALF, WIDTH), BF16),
            pltpu.SemaphoreType.DMA((messages,)),
            pltpu.SemaphoreType.DMA((messages,)),
            pltpu.SemaphoreType.DMA((CHUNKS * 2,)),
        ],
        compiler_params=pltpu.CompilerParams(
            collective_id=0, has_side_effects=True, vmem_limit_bytes=63 * 1024 * 1024),
    )(tokens, gate_weight, up_weight, down_weight)


def solution(mesh):
    return jax.shard_map(
        on_device,
        mesh=mesh,
        in_specs=(
            P(("dp", "col"), "row"),
            P("row", ("dp", "col")),
            P("row", ("dp", "col")),
            P(("dp", "col"), "row"),
        ),
        out_specs=P(("dp", "col"), "row"),
        check_vma=False,
    )
```

```python
import functools

import jax
import jax.numpy as jnp
from jax import lax
from jax.experimental import pallas as pl
from jax.experimental.pallas import tpu as pltpu
from jax.sharding import PartitionSpec as P

MESH = pl.DeviceIdType.MESH
F32 = jnp.float32
BF16 = jnp.bfloat16

CHUNKS = 4
BLOCK = 128
HALF = BLOCK // CHUNKS // 2
UNITS = 448
TAIL = 64
MAIN = 384
PACKED = 896
PADDED = 512
WIDTH = 1024
MESSAGES = 36


def kernel(tokens_hbm, gate_hbm, up_hbm, down_hbm, out_hbm,
           tokens_ref, out_ref, weights, tok, w, d, part, pair, chain_in, chain_out, hid, term,
           in_far, in_near, in_far2, in_near2, z_send, z_in,
           send_sem, recv_sem, local_sem, load_sem, store_sem):
    load_tokens = pltpu.make_async_copy(tokens_hbm, tokens_ref, load_sem.at[0])
    load_tokens.start()
    x = lax.axis_index("dp")
    row = lax.axis_index("row")
    col = lax.axis_index("col")
    z, core = row // 2, row % 2
    zh, y = col // 4, col % 4

    def shift(value, by):
        return lax.rem(value + (by + 4), 4)

    core_peer = {"row": row + 1 - 2 * core}
    zh_peer = {"col": (1 - zh) * 4 + y}
    def ring(by_x, by_y):
        return {"dp": lax.rem(x + (by_x + 4), 4), "col": zh * 4 + lax.rem(y + (by_y + 4), 4)}

    near = z // 2

    barrier = pltpu.get_barrier_semaphore()
    for peer in (core_peer, zh_peer, ring(1, 0), ring(-1, 0), ring(0, 1), ring(0, -1)):
        pl.semaphore_signal(barrier, inc=1, device_id=peer, device_id_type=MESH)

    @pl.when(z > 0)
    def _():
        pl.semaphore_signal(barrier, inc=1, device_id={"row": row - 2}, device_id_type=MESH)

    @pl.when(z < 3)
    def _():
        pl.semaphore_signal(barrier, inc=1, device_id={"row": row + 2}, device_id_type=MESH)

    loads = [
        pltpu.make_async_copy(src, dst, load_sem.at[1 + i])
        for i, (src, dst) in enumerate((
            (gate_hbm.at[:MAIN], weights.at[:MAIN]),
            (up_hbm.at[:MAIN], weights.at[MAIN:2 * MAIN]),
            (gate_hbm.at[MAIN:], weights.at[2 * MAIN:2 * MAIN + TAIL]),
            (up_hbm.at[MAIN:], weights.at[2 * MAIN + TAIL:]),
            (down_hbm, d.at[:UNITS]),
        ))
    ]
    for load in loads:
        load.start()
    d[UNITS:] = jnp.zeros((PADDED - UNITS, WIDTH), BF16)

    at_end = jnp.logical_or(z == 0, z == 3)

    @pl.when(at_end)
    def _():
        pl.semaphore_wait(barrier, 7)

    @pl.when(jnp.logical_not(at_end))
    def _():
        pl.semaphore_wait(barrier, 8)

    load_tokens.wait()
    sent = []
    stores = []

    def copy(src, dst, index, peer):
        place = index[0] + index[1]
        return pltpu.make_async_remote_copy(
            src_ref=src, dst_ref=dst, send_sem=send_sem.at[place], recv_sem=recv_sem.at[place],
            device_id=peer, device_id_type=MESH)

    def send(src, dst, index, peer, guard=None):
        copy(src, dst, index, peer).start()
        sent.append((src, dst, index, peer, guard))

    def arrived(dst, index, peer):
        copy(dst, dst, index, peer).wait_recv()

    tasks = []

    def add(run, guard=None):
        tasks.append((run, guard))

    def one(c, n):
        o = n + near - 2 * n * near
        swap = o
        base = (c * 2 + o) * MESSAGES
        first, second = x + swap * (y - x), y + swap * (x - y)
        first_peer = {way: ring((1 - swap) * way, swap * way) for way in (1, -1)}
        second_peer = {way: ring(swap * way, (1 - swap) * way) for way in (1, -1)}
        lo = pl.multiple_of((c * 2 + o) * HALF, HALF)
        mine = tokens_ref.at[pl.ds(lo, HALF)]
        here = tok.at[c, o]
        f = {k: shift(first, k) for k in (-1, 0, 1, 2)}
        s = {k: shift(second, k) for k in (-1, 0, 1, 2)}
        local = pltpu.make_async_copy(mine, here.at[s[0], f[0], zh], local_sem.at[c * 2 + o])

        def begin():
            send(mine, here.at[s[0], f[0], zh], (base, 0), zh_peer)
            for i, way in enumerate((1, -1)):
                send(mine, here.at[s[0], f[0], zh], (base, 1 + i), first_peer[way])
            local.start()

        def other_half():
            block = here.at[s[0], f[0], 1 - zh]
            arrived(block, (base, 0), zh_peer)
            for i, way in enumerate((1, -1)):
                send(block, block, (base, 3 + i), first_peer[way])

        def forward_own():
            block = here.at[s[0], f[-1], zh]
            arrived(block, (base, 1), first_peer[-1])
            send(block, block, (base, 5), first_peer[1])

        def forward_other():
            block = here.at[s[0], f[1], 1 - zh]
            arrived(block, (base, 4), first_peer[1])
            send(block, block, (base, 6), first_peer[-1])

        def second_axis():
            arrived(here.at[s[0], f[1], zh], (base, 2), first_peer[1])
            arrived(here.at[s[0], f[-1], 1 - zh], (base, 3), first_peer[-1])
            arrived(here.at[s[0], f[2], zh], (base, 5), first_peer[-1])
            arrived(here.at[s[0], f[2], 1 - zh], (base, 6), first_peer[1])
            local.wait()
            for i, way in enumerate((1, -1)):
                send(here.at[s[0]], here.at[s[0]], (base, 7 + i), second_peer[way])

        def forward_second(way):
            lower = 0 if way == 1 else 2

            def run():
                arrived(here.at[s[-way]], (base, (7 if way == 1 else 8)), second_peer[-way])
                block = here.at[s[-way], lower:lower + 2]
                send(block, block, (base, (9 if way == 1 else 10)), second_peer[way])

            return run

        add(begin)
        add(other_half)
        add(forward_own)
        add(forward_other)
        add(second_axis)
        add(forward_second(1))
        add(forward_second(-1))

        p = z + o * (3 - 2 * z)
        on = [p == position for position in range(4)]
        onward, backward = {"row": row + 2 - 4 * o}, {"row": row - 2 + 4 * o}

        def tile(k):
            key = k if k < 3 else -1
            rows = 4 * HALF
            own = part.at[c, o, k, :, core]
            away = part.at[c, o, k, :, 1 - core]
            pair_in = pair.at[c, o, k]
            incoming = chain_in.at[c, o, k]
            outgoing = chain_out.at[c, o, k]
            hidden = hid.at[c, o, k, core]
            hidden_away = hid.at[c, o, k, 1 - core]

            def gate_up():
                if k == 2:
                    arrived(here.at[s[2], 0:2], (base, 9), second_peer[-1])
                    arrived(here.at[s[2], 2:4], (base, 10), second_peer[1])
                a = here[s[key]].reshape(2 * rows, WIDTH)
                both = jnp.dot(a, w[...], preferred_element_type=F32).astype(BF16)
                part[c, o, k] = both.reshape(4, 2, HALF, PACKED)
                send(away, pair_in, (base, 11 + k), core_peer)

            def total(with_chain):
                value = own[...].astype(F32).reshape(rows, PACKED) + pair_in[...].astype(F32).reshape(rows, PACKED)
                if with_chain:
                    value = value + incoming[...].astype(F32)
                return value

            def link(position):
                def run():
                    arrived(pair_in, (base, 11 + k), core_peer)
                    if position:
                        arrived(incoming, (base, 15 + k), backward)
                    value = total(position > 0)
                    if position < 3:
                        outgoing[...] = value.astype(BF16)
                        send(outgoing, incoming, (base, 15 + k), onward, on[position])
                    else:
                        g, u = value[:, :MAIN], value[:, MAIN:2 * MAIN]
                        last = value[:, 2 * MAIN:]
                        turned = pltpu.roll(last, 64, 1)
                        lane = lax.broadcasted_iota(jnp.int32, (rows // 2, 128), 1)
                        main = (jax.nn.silu(g) * u).astype(BF16)
                        for j in range(3):
                            hidden[2 * j:2 * j + 2] = main[:, j * 128:(j + 1) * 128].reshape(2, rows // 2, 128)
                        tail = jax.nn.silu(last) * turned
                        other = pltpu.roll(tail[rows // 2:], 64, 1)
                        hidden[6] = jnp.where(lane < TAIL, tail[:rows // 2], other).astype(BF16)
                        send(hidden, hidden, (base, 19 + k), backward, on[position])
                        send(hidden, hidden, (base, 23 + k), core_peer, on[position])
                return run

            def spread(position):
                def run():
                    arrived(hidden, (base, 19 + k), onward)
                    if position:
                        send(hidden, hidden, (base, 19 + k), backward, on[position])
                    send(hidden, hidden, (base, 23 + k), core_peer, on[position])
                return run

            def down():
                arrived(hidden_away, (base, 23 + k), core_peer)
                halves = []
                for h in range(2):
                    tail = hid[c, o, k, h, 6]
                    other = pltpu.roll(tail.astype(F32), 64, 1).astype(BF16)
                    tiles = [hid[c, o, k, h, 2 * j:2 * j + 2].reshape(rows, 128) for j in range(3)]
                    tiles.append(jnp.concatenate((tail, other), axis=0))
                    halves.append(jnp.concatenate(tiles, axis=1))
                a = jnp.concatenate(halves, axis=0)
                term[c, o, k] = jnp.dot(a, d[...], preferred_element_type=F32).astype(BF16).reshape(2, 4, HALF, WIDTH)

            def out_far():
                for i, way in enumerate((1, -1)):
                    send(term.at[c, o, 2, i], in_far.at[c, o, i], (base, 27 + i), second_peer[way])

            def out_near():
                i, way = (0, 1) if k == 1 else (1, -1)
                arrived(in_far.at[c, o, i], (base, 27 + i), second_peer[-way])
                term[c, o, k, i] = (term[c, o, k, i].astype(F32) + in_far[c, o, i].astype(F32)).astype(BF16)
                send(term.at[c, o, k], in_near.at[c, o, i], (base, 29 + i), second_peer[way])

            add(gate_up)
            for position in range(2 - 2 * (1 - n), 4 - 2 * (1 - n)):
                add(link(position), on[position])
            for position in (2, 1, 0):
                if position // 2 == n:
                    add(spread(position), on[position])
            add(down)
            return out_far if k == 2 else out_near

        outs = [tile(k) for k in range(4)]
        for k in (2, 1, 3):
            add(outs[k])

        def out_second():
            for i, way in enumerate((1, -1)):
                arrived(in_near.at[c, o, i], (base, 29 + i), second_peer[-way])
            value = term[c, o, 0].astype(F32) + in_near[c, o, 0].astype(F32) + in_near[c, o, 1].astype(F32)
            term[c, o, 0] = value.astype(BF16)
            for i, way in enumerate((1, -1)):
                send(term.at[c, o, 0, i, f[2]], in_far2.at[c, o, i], (base, 31 + i), first_peer[way])

        def out_first():
            for i, way in enumerate((1, -1)):
                arrived(in_far2.at[c, o, i], (base, 31 + i), first_peer[-way])
                block = term.at[c, o, 0, i, f[way]]
                block[...] = (block[...].astype(F32) + in_far2[c, o, i].astype(F32)).astype(BF16)
                send(term.at[c, o, 0, :, f[way]], in_near2.at[c, o, i], (base, 33 + i), first_peer[way])

        def out_zh():
            for i, way in enumerate((1, -1)):
                arrived(in_near2.at[c, o, i], (base, 33 + i), first_peer[-way])
            z_send[c, o] = (term[c, o, 0, :, f[0]].astype(F32) + in_near2[c, o, 0].astype(F32)
                            + in_near2[c, o, 1].astype(F32)).astype(BF16)
            send(z_send.at[c, o, 1 - zh], z_in.at[c, o], (base, 35), zh_peer)

        def out_end():
            arrived(z_in.at[c, o], (base, 35), zh_peer)
            rows = pl.ds(lo, HALF)
            out_ref[rows] = (z_send[c, o, zh].astype(F32) + z_in[c, o].astype(F32)).astype(BF16)
            store = (out_ref.at[rows], out_hbm.at[rows], store_sem.at[c * 2 + o])
            pltpu.make_async_copy(*store).start()
            stores.append(store)

        add(out_second)
        add(out_first)
        add(out_zh)
        add(out_end)

    def pack():
        for load in loads:
            load.wait()

        def turn(i, carry):
            start = pl.multiple_of(i * 128, 128)
            w[:, pl.ds(start, 128)] = weights[pl.ds(start, 128), :].T
            return carry

        lax.fori_loop(0, PACKED // 128, turn, 0)

    for c in range(CHUNKS):
        for n in range(2):
            one(c, n)
    for place, number in enumerate(ORDER):
        if place == PACK:
            pack()
        run, guard = tasks[number]
        if guard is None:
            run()
        else:
            pl.when(guard)(run)

    for store in stores:
        pltpu.make_async_copy(*store).wait()
    for src, dst, index, peer, guard in sent:
        def finish(item=(src, dst, index, peer)):
            copy(*item).wait_send()

        if guard is None:
            finish()
        else:
            pl.when(guard)(finish)


PACK = 4
ORDER = (
    0, 72, 38, 110, 182, 144, 146, 216, 112, 184, 254, 1, 2, 218, 40, 74, 256, 3, 73, 39,
    41, 111, 75, 4, 7, 8, 183, 145, 147, 9, 113, 217, 76, 79, 80, 42, 45, 46, 5, 25,
    26, 185, 6, 13, 14, 81, 148, 255, 27, 151, 152, 114, 117, 47, 15, 77, 43, 97, 98, 60,
    19, 20, 78, 85, 86, 48, 44, 50, 49, 51, 149, 169, 170, 186, 99, 116, 150, 157, 158, 219,
    21, 61, 118, 257, 87, 115, 91, 92, 52, 122, 153, 132, 133, 62, 55, 163, 258, 171, 188, 56,
    164, 57, 220, 223, 224, 194, 123, 124, 93, 187, 204, 127, 205, 206, 63, 64, 28, 29, 259, 134,
    58, 165, 128, 129, 222, 229, 221, 241, 242, 53, 10, 189, 22, 159, 23, 199, 24, 31, 200, 59,
    201, 65, 125, 235, 261, 207, 260, 266, 236, 16, 190, 17, 191, 130, 225, 131, 137, 30, 33, 135,
    18, 32, 54, 172, 230, 88, 66, 89, 195, 196, 202, 203, 209, 67, 94, 95, 243, 126, 138, 136,
    139, 271, 166, 237, 167, 119, 96, 276, 103, 100, 277, 101, 278, 208, 211, 168, 231, 175, 90, 104,
    192, 102, 105, 272, 273, 197, 198, 210, 160, 161, 173, 174, 177, 162, 176, 120, 267, 268, 193, 121,
    140, 82, 83, 274, 68, 275, 281, 238, 11, 12, 34, 262, 239, 240, 247, 212, 279, 280, 283, 269,
    270, 282, 141, 263, 244, 245, 69, 84, 106, 232, 233, 213, 246, 249, 234, 248, 154, 155, 156, 178,
    35, 264, 265, 284, 226, 214, 70, 142, 179, 227, 107, 36, 228, 250, 180, 285, 251, 108, 286, 252,
    143, 215, 181, 109, 71, 287, 37, 253,
)


def on_device(tokens, gate_weight, up_weight, down_weight):
    hbm = pl.BlockSpec(memory_space=pl.ANY)
    c2 = (CHUNKS, 2)
    messages = CHUNKS * 2 * MESSAGES
    return pl.pallas_call(
        kernel,
        out_shape=jax.ShapeDtypeStruct(tokens.shape, BF16),
        in_specs=[hbm] * 4,
        out_specs=hbm,
        scratch_shapes=[
            pltpu.VMEM((BLOCK, WIDTH), BF16),
            pltpu.VMEM((BLOCK, WIDTH), BF16),
            pltpu.VMEM((PACKED, WIDTH), BF16),
            pltpu.VMEM(c2 + (4, 4, 2, HALF, WIDTH), BF16),
            pltpu.VMEM((WIDTH, PACKED), BF16),
            pltpu.VMEM((PADDED, WIDTH), BF16),
            pltpu.VMEM(c2 + (4, 4, 2, HALF, PACKED), BF16),
            pltpu.VMEM(c2 + (4, 4, HALF, PACKED), BF16),
            pltpu.VMEM(c2 + (4, 4 * HALF, PACKED), BF16),
            pltpu.VMEM(c2 + (4, 4 * HALF, PACKED), BF16),
            pltpu.VMEM(c2 + (4, 2, 7, 2 * HALF, 128), BF16),
            pltpu.VMEM(c2 + (4, 2, 4, HALF, WIDTH), BF16),
            pltpu.VMEM(c2 + (2, 4, HALF, WIDTH), BF16),
            pltpu.VMEM(c2 + (2, 2, 4, HALF, WIDTH), BF16),
            pltpu.VMEM(c2 + (2, HALF, WIDTH), BF16),
            pltpu.VMEM(c2 + (2, 2, HALF, WIDTH), BF16),
            pltpu.VMEM(c2 + (2, HALF, WIDTH), BF16),
            pltpu.VMEM(c2 + (HALF, WIDTH), BF16),
            pltpu.SemaphoreType.DMA((messages,)),
            pltpu.SemaphoreType.DMA((messages,)),
            pltpu.SemaphoreType.DMA((CHUNKS * 2,)),
            pltpu.SemaphoreType.DMA((6,)),
            pltpu.SemaphoreType.DMA((CHUNKS * 2,)),
        ],
        compiler_params=pltpu.CompilerParams(
            collective_id=0, has_side_effects=True, vmem_limit_bytes=63 * 1024 * 1024),
    )(tokens, gate_weight.T, up_weight.T, down_weight)


def solution(mesh):
    return jax.shard_map(
        on_device,
        mesh=mesh,
        in_specs=(
            P(("dp", "col"), "row"),
            P("row", ("dp", "col")),
            P("row", ("dp", "col")),
            P(("dp", "col"), "row"),
        ),
        out_specs=P(("dp", "col"), "row"),
        check_vma=False,
    )
```
